32 devices in a mesh: groups: 2 (over x), ctx: 16 (over z, y, core).
Axes of the slice: x: 2, y: 2, z: 4, core: 2. Of those that a mesh axis runs over, the one named last changes fastest.
Arguments:
- queries: bfloat16 [4096, 8192], P(('groups', 'ctx')), parts along dimension 0, may hold values from -8 to 8
- new_keys: bfloat16 [4096, 1024], P(('groups', 'ctx')), parts along dimension 0, may hold values from -12 to 12
- new_values: bfloat16 [4096, 1024], P(('groups', 'ctx')), parts along dimension 0, may hold values from -6 to 6
- prefix_keys: bfloat16 [256, 1024], P(('groups', 'ctx')), parts along dimension 0, may hold values from -16 to 16
- prefix_values: bfloat16 [256, 1024], P(('groups', 'ctx')), parts along dimension 0, may hold values from -6 to 6
- pool_keys: bfloat16 [32, 2, 256, 1024], P(('groups', 'ctx')), parts along dimension 0, may hold values from -12 to 12
- pool_values: bfloat16 [32, 2, 256, 1024], P(('groups', 'ctx')), parts along dimension 0, may hold values from -6 to 6
- owners: int32 [4], P('groups'), parts along dimension 0, may hold values from 0 to 15
- lengths: int32 [32], P(('groups', 'ctx')), parts along dimension 0, may hold values from 1 to 128, as said below
Outputs:
- attended: bfloat16 [4096, 8192], P(('groups', 'ctx')), parts along dimension 0
The draws below stay inside these ranges and needn't reach their ends.
There are 2 independent parts, one for each index of `groups`. The reference program is written for one: setup_inputs(seed, part) draws one part's arguments, and reference() takes and returns one part's arrays. A program takes and returns all parts, laid end to end along the dimension named above; each array names one. Nothing has to cross between parts.
Inputs may be any that keep to these rules, and one draw needn't show every extreme that they name: `lengths`: some device's prompt fills all 128 slots.
All inputs are finite; a program needn't handle non-finite values.
Results may differ from the reference program's by a relative error of at most 0.0035.
Values may be sent and summed in bfloat16 or wider, within the bound.
A program may use at most 128 MiB of HBM per device.

```python
import jax
import jax.numpy as jnp
from jax import lax

H = 64
KVH = 8
HD = 128
Q_DEV = 128
SB = 2
BLK = 256
PREFIX = 128
TOKENS = 2048
N_CTX = 16


def draw_queries(key, part):
    noise_key = jax.random.fold_in(key, 11)
    values_drawn = jnp.clip(1.5 * jax.random.normal(noise_key, (TOKENS, H * HD), jnp.float32), -8.0, 8.0)
    return values_drawn.astype(jnp.bfloat16)


def draw_prefix_keys(key, part):
    noise_key = jax.random.fold_in(key, 13)
    values_drawn = jnp.clip(2.0 * jax.random.normal(noise_key, (PREFIX, KVH * HD), jnp.float32), -16.0, 16.0)
    return values_drawn.astype(jnp.bfloat16)


def draw_lengths(key, part):
    key_values, key_full = jax.random.split(jax.random.fold_in(key, 23))
    count = TOKENS // Q_DEV
    drawn = jax.random.randint(key_values, (count,), 1, Q_DEV + 1)
    full_index = jax.random.randint(key_full, (), 0, count)
    return drawn.at[full_index].set(Q_DEV).astype(jnp.int32)


def levels(rng, dims, shards, smallest, top_value):
    def one(dim, parts):
        steps = jax.random.uniform(jax.random.fold_in(jax.random.fold_in(rng, 6), dim), (parts,), jnp.float32, smallest / len(shards), top_value / len(shards))
        return jnp.repeat(jnp.exp(steps), dims[dim] // parts).reshape((-1,) + (1,) * (len(dims) - dim - 1))

    gain = one(*shards[0])
    for cut in shards[1:]:
        gain = gain * one(*cut)
    return gain


def centred(own_key, shape, spread, most, cuts=(), kind=jnp.bfloat16):
    entries = spread * jax.random.normal(own_key, shape, jnp.float32)
    if cuts:
        entries = entries * levels(own_key, shape, cuts, -0.22, 0.18)
    return jnp.clip(entries, -most, most).astype(kind)


def setup_inputs(seed: int = 0, part: int = 0) -> dict:
    seeds = jax.random.split(jax.random.key(seed), 10)
    part_splits = jax.random.split(jax.random.fold_in(seeds[9], part), 10)
    return {
        "queries": draw_queries(jax.random.fold_in(jax.random.fold_in(seeds[9], part), 71), part),
        "new_keys": centred(part_splits[1], (TOKENS, KVH * HD), 2.0, 12.0, ((0, 16),)),
        "new_values": centred(part_splits[2], (TOKENS, KVH * HD), 1.0, 6.0, ((0, 16),)),
        "prefix_keys": draw_prefix_keys(jax.random.fold_in(jax.random.fold_in(seeds[9], part), 71), part),
        "prefix_values": centred(part_splits[4], (PREFIX, KVH * HD), 1.0, 6.0, ((0, 16),)),
        "pool_keys": centred(part_splits[5], (N_CTX, SB, BLK, KVH * HD), 2.0, 12.0, ((0, 16),)),
        "pool_values": centred(part_splits[6], (N_CTX, SB, BLK, KVH * HD), 1.0, 6.0, ((0, 16),)),
        "owners": jax.random.randint(part_splits[7], (SB,), 0, N_CTX).astype(jnp.int32),
        "lengths": draw_lengths(jax.random.fold_in(jax.random.fold_in(seeds[9], part), 71), part),
    }


def reference(queries, new_keys, new_values, prefix_keys, prefix_values, pool_keys, pool_values, owners, lengths):
    group_size = H // KVH
    score_scale = 1.0 / (HD ** 0.5)
    block_ids = jnp.arange(SB).astype(jnp.int32)
    shared_keys = pool_keys[owners.astype(jnp.int32), block_ids].reshape(SB * BLK, KVH * HD)
    shared_values = pool_values[owners.astype(jnp.int32), block_ids].reshape(SB * BLK, KVH * HD)

    def one_block(device):
        start = (device * Q_DEV).astype(jnp.int32)
        query_rows = lax.dynamic_slice_in_dim(queries, start, Q_DEV, 0)
        own_keys = lax.dynamic_slice_in_dim(new_keys, start, Q_DEV, 0)
        own_values = lax.dynamic_slice_in_dim(new_values, start, Q_DEV, 0)
        length = lengths[device]
        key_rows = jnp.concatenate([shared_keys, prefix_keys, own_keys], axis=0)
        value_rows = jnp.concatenate([shared_values, prefix_values, own_values], axis=0)
        positions = jnp.arange(Q_DEV).astype(jnp.int32)
        own_visible = (positions[None, :] <= positions[:, None]) & (positions[None, :] < length)
        visible = jnp.concatenate([jnp.ones((Q_DEV, SB * BLK + PREFIX), dtype=bool), own_visible], axis=1)
        visible = jnp.repeat(visible, group_size, axis=0)
        pieces = []
        for kv_head in range(KVH):
            head_queries = query_rows[:, kv_head * group_size * HD:(kv_head + 1) * group_size * HD].reshape(Q_DEV * group_size, HD)
            head_keys = key_rows[:, kv_head * HD:(kv_head + 1) * HD]
            head_values = value_rows[:, kv_head * HD:(kv_head + 1) * HD]
            scores = lax.dot_general(head_queries, head_keys, (((1,), (1,)), ((), ())), preferred_element_type=jnp.float32) * score_scale
            scores = jnp.where(visible, scores, -1e30)
            row_max = jnp.max(scores, axis=1, keepdims=True)
            weights = jnp.where(visible, jnp.exp(scores - row_max), 0.0)
            totals = jnp.sum(weights, axis=1, keepdims=True)
            summed = jnp.dot(weights.astype(jnp.bfloat16), head_values, preferred_element_type=jnp.float32)
            pieces.append((summed / totals).reshape(Q_DEV, group_size * HD))
        joined = jnp.concatenate(pieces, axis=1)
        live = positions < length
        return jnp.where(live[:, None], joined, 0.0).astype(jnp.bfloat16)

    blocks = lax.map(one_block, jnp.arange(TOKENS // Q_DEV).astype(jnp.int32))
    return blocks.reshape(TOKENS, H * HD)
```

```python
import functools

import jax
import jax.numpy as jnp
from jax import lax
from jax.experimental import pallas as pl
from jax.experimental.pallas import tpu as pltpu
from jax.sharding import PartitionSpec as P

HD = 128
SIB_STEPS = 1
HOP_STEPS = 2
HEADS_AT_ONCE = 4


def grid_of(ring):
    chips = ring // 2
    short = 1
    while (short * 2) ** 2 <= chips and chips % (short * 2) == 0:
        short *= 2
    return chips // short, short


def kernel(
    ring, heads, kv_heads,
    q_ref, nk_ref, nv_ref, pk_ref, pv_ref, poolk_ref, poolv_ref, owners_ref, lengths_ref,
    out_ref,
    x, sib_s, sib_r, yu_s, yu_r, yd_s, yd_r, xy, zu_s, zu_r, zd_s, zd_r, kvf, bias,
    send_sems, recv_sems,
):
    long, short = grid_of(ring)
    me = lax.axis_index("ctx")
    core = lax.rem(me, 2)
    chip = lax.div(me, 2)
    py = lax.rem(chip, short)
    pz = lax.div(chip, short)
    sibling = me + 1 - 2 * core
    blocks, blk = poolk_ref.shape[1], poolk_ref.shape[2]
    chunks = kv_heads * blocks
    own_rows = pk_ref.shape[0]
    pre = own_rows * ring // blocks
    rows = q_ref.shape[0]
    group = heads // kv_heads

    barrier = pltpu.get_barrier_semaphore()

    def greet(target):
        pl.semaphore_signal(barrier, inc=1, device_id={"ctx": target})

    greet(sibling)
    for pos, size, step in ((py, short, 2), (pz, long, 2 * short)):
        @pl.when(pos > 0)
        def _():
            greet(me - step)

        @pl.when(pos < size - 1)
        def _():
            greet(me + step)

    peers = 1
    for pos, size in ((py, short), (pz, long)):
        peers = peers + jnp.where(pos > 0, 1, 0) + jnp.where(pos < size - 1, 1, 0)
    pl.semaphore_wait(barrier, peers)

    def remote(kind, i, src, dst, target):
        return pltpu.make_async_remote_copy(
            src_ref=src, dst_ref=dst, send_sem=send_sems.at[kind, i], recv_sem=recv_sems.at[kind, i],
            device_id={"ctx": target}, device_id_type=pl.DeviceIdType.MESH,
        )

    length = lengths_ref[0]
    tok = lax.broadcasted_iota(jnp.int32, (rows, rows), 0)
    key = lax.broadcasted_iota(jnp.int32, (rows, rows), 1)
    bias[...] = jnp.where((key <= tok) & (key < length), 0.0, -1e30)

    def cols(g):
        return pl.ds(pl.multiple_of(g * HD, HD), HD)

    def build(i):
        g, b = lax.div(i, blocks), lax.rem(i, blocks)
        mine = jnp.where(owners_ref[b] == me, 1.0, 0.0).astype(jnp.float32)
        row = lax.broadcasted_iota(jnp.int32, (pre, HD), 0) + b * pre
        in_mine = (row >= me * own_rows) & (row < (me + 1) * own_rows)
        parts = []
        for pool, pre_ref in ((poolk_ref, pk_ref), (poolv_ref, pv_ref)):
            page = pool[0, b, :, cols(g)]
            page = page * jnp.full(page.shape, mine, jnp.float32).astype(jnp.bfloat16)
            mine_pre = pre_ref[:, cols(g)].astype(jnp.float32)
            tiled = jnp.concatenate([mine_pre] * (pre // own_rows), axis=0)
            parts.append((page, jnp.where(in_mine, tiled, 0.0).astype(jnp.bfloat16)))
        is_k = core == 0

        @pl.when(is_k)
        def _():
            x[i, :blk], x[i, blk:] = parts[0]
            sib_s[i, :blk], sib_s[i, blk:] = parts[1]

        @pl.when(jnp.logical_not(is_k))
        def _():
            x[i, :blk], x[i, blk:] = parts[1]
            sib_s[i, :blk], sib_s[i, blk:] = parts[0]

    def valid(i):
        return (i >= 0) & (i < chunks)

    def scan(t, kind, pos, size, step, base, src, up_s, up_r, dn_s, dn_r, write):
        up = t - base - pos * HOP_STEPS

        @pl.when(valid(up))
        def _():
            @pl.when(pos > 0)
            def _():
                remote(kind, up, up_s.at[up], up_r.at[up], me - step).wait_recv()

            @pl.when((pos > 0) & (pos < size - 1))
            def _():
                up_s[up] = src[up] + up_r[up]

            @pl.when((pos == 0) & (pos < size - 1))
            def _():
                up_s[up] = src[up]

            @pl.when(pos < size - 1)
            def _():
                remote(kind, up, up_s.at[up], up_r.at[up], me + step).start()

        dn = t - base - (size - 1 - pos) * HOP_STEPS

        @pl.when(valid(dn))
        def _():
            @pl.when(pos < size - 1)
            def _():
                remote(kind + 1, dn, dn_s.at[dn], dn_r.at[dn], me + step).wait_recv()

            @pl.when((pos > 0) & (pos < size - 1))
            def _():
                dn_s[dn] = src[dn] + dn_r[dn]

            @pl.when((pos > 0) & (pos == size - 1))
            def _():
                dn_s[dn] = src[dn]

            @pl.when(pos > 0)
            def _():
                remote(kind + 1, dn, dn_s.at[dn], dn_r.at[dn], me - step).start()

        end = t - base - (size - 1) * HOP_STEPS

        @pl.when(valid(end))
        def _():
            @pl.when((pos > 0) & (pos < size - 1))
            def _():
                write(end, src[end] + up_r[end] + dn_r[end])

            @pl.when((pos > 0) & (pos == size - 1))
            def _():
                write(end, src[end] + up_r[end])

            @pl.when((pos == 0) & (pos < size - 1))
            def _():
                write(end, src[end] + dn_r[end])

            if size == 1:
                write(end, src[end])

        return base + (size - 1) * HOP_STEPS

    live = lax.broadcasted_iota(jnp.int32, (rows, HD), 0) < length
    batches = group // HEADS_AT_ONCE
    score_scale = 1.0 / HD**0.5
    all_rows = blocks * (blk + pre)

    def attend(m):
        g, part = lax.div(m, batches), lax.rem(m, batches)
        first = g * group + part * HEADS_AT_ONCE
        q = jnp.concatenate([q_ref[:, cols(first + j)] for j in range(HEADS_AT_ONCE)], axis=0)
        keys = kvf[0, pl.ds(g * blocks, blocks)].reshape(all_rows, HD)
        values = kvf[1, pl.ds(g * blocks, blocks)].reshape(all_rows, HD)
        dims = (((1,), (1,)), ((), ()))
        s_far = lax.dot_general(q, keys, dims, preferred_element_type=jnp.float32) * score_scale
        s_own = lax.dot_general(q, nk_ref[:, cols(g)], dims, preferred_element_type=jnp.float32)
        s_own = s_own * score_scale + jnp.concatenate([bias[...]] * HEADS_AT_ONCE, axis=0)
        top = jnp.maximum(jnp.max(s_far, axis=1, keepdims=True), jnp.max(s_own, axis=1, keepdims=True))
        w_far = jnp.exp(s_far - top).astype(jnp.bfloat16)
        w_own = jnp.exp(s_own - top).astype(jnp.bfloat16)
        v_far = jnp.concatenate([values, jnp.ones_like(values)], axis=1)
        own = nv_ref[:, cols(g)]
        v_own = jnp.concatenate([own, jnp.ones_like(own)], axis=1)
        summed = jnp.dot(w_far, v_far, preferred_element_type=jnp.float32)
        summed += jnp.dot(w_own, v_own, preferred_element_type=jnp.float32)
        result = summed[:, :HD] / summed[:, HD:]
        for j in range(HEADS_AT_ONCE):
            piece = jnp.where(live, result[j * rows : (j + 1) * rows], 0.0)
            out_ref[:, cols(first + j)] = piece.astype(out_ref.dtype)

    def finish(i, value):
        kvf[core, i] = value
        remote(5, i, kvf.at[core, i], kvf.at[core, i], sibling).start()

    y_base = SIB_STEPS
    z_base = y_base + (short - 1) * HOP_STEPS
    f_base = z_base + (long - 1) * HOP_STEPS
    c_base = f_base + SIB_STEPS
    attends = kv_heads * batches
    steps = c_base + max(chunks + 1, attends + blocks)

    def one_step(t, carry):
        @pl.when(t < chunks)
        def _():
            build(t)
            remote(0, t, sib_s.at[t], sib_r.at[t], sibling).start()

        i = t - y_base

        @pl.when(valid(i))
        def _():
            remote(0, i, sib_s.at[i], sib_r.at[i], sibling).wait_recv()
            x[i] = x[i] + sib_r[i]

        def write_xy(i, value):
            xy[i] = value

        scan(t, 1, py, short, 2, y_base, x, yu_s, yu_r, yd_s, yd_r, write_xy)
        scan(t, 3, pz, long, 2 * short, z_base, xy, zu_s, zu_r, zd_s, zd_r, finish)
        i_c = t - c_base

        @pl.when(valid(i_c))
        def _():
            remote(5, i_c, kvf.at[core, i_c], kvf.at[1 - core, i_c], sibling).wait_recv()

        m = t - c_base - (blocks - 1)

        @pl.when((m >= 0) & (m < attends))
        def _():
            attend(m)

        return carry

    lax.fori_loop(0, steps, one_step, 0)

    def drain(i, carry):
        remote(0, i, sib_s.at[i], sib_r.at[i], sibling).wait_send()
        remote(5, i, kvf.at[core, i], kvf.at[core, i], sibling).wait_send()
        for kind, pos, size, step, up_s, up_r, dn_s, dn_r in (
            (1, py, short, 2, yu_s, yu_r, yd_s, yd_r),
            (3, pz, long, 2 * short, zu_s, zu_r, zd_s, zd_r),
        ):
            @pl.when(pos < size - 1)
            def _():
                remote(kind, i, up_s.at[i], up_r.at[i], me + step).wait_send()

            @pl.when(pos > 0)
            def _():
                remote(kind + 1, i, dn_s.at[i], dn_r.at[i], me - step).wait_send()

        return carry

    lax.fori_loop(0, chunks, drain, 0)


def solution(mesh):
    ring = mesh.shape["ctx"]

    def body(queries, new_keys, new_values, prefix_keys, prefix_values, pool_keys, pool_values, owners, lengths):
        heads = queries.shape[1] // HD
        kv_heads = new_keys.shape[1] // HD
        blocks, blk = pool_keys.shape[1], pool_keys.shape[2]
        chunks = kv_heads * blocks
        c_rows = blk + prefix_keys.shape[0] * ring // blocks
        chunk_buf = pltpu.VMEM((chunks, c_rows, HD), jnp.bfloat16)
        vm = pl.BlockSpec(memory_space=pltpu.VMEM)
        sm = pl.BlockSpec(memory_space=pltpu.SMEM)
        return pl.pallas_call(
            functools.partial(kernel, ring, heads, kv_heads),
            out_shape=jax.ShapeDtypeStruct(queries.shape, jnp.bfloat16),
            in_specs=[vm] * 7 + [sm] * 2,
            out_specs=vm,
            scratch_shapes=[chunk_buf] * 12
            + [
                pltpu.VMEM((2, chunks, c_rows, HD), jnp.bfloat16),
                pltpu.VMEM((queries.shape[0], queries.shape[0]), jnp.float32),
                pltpu.SemaphoreType.DMA((6, chunks)),
                pltpu.SemaphoreType.DMA((6, chunks)),
            ],
            compiler_params=pltpu.CompilerParams(
                collective_id=0, has_side_effects=True, vmem_limit_bytes=67043328
            ),
        )(queries, new_keys, new_values, prefix_keys, prefix_values, pool_keys, pool_values, owners, lengths)

    two = P(("groups", "ctx"), None)
    four = P(("groups", "ctx"), None, None, None)
    return jax.shard_map(
        body, mesh=mesh, in_specs=(two,) * 5 + (four,) * 2 + (P("groups"), P(("groups", "ctx"))),
        out_specs=two, check_vma=False,
    )
```

```python
import functools

import jax
import jax.numpy as jnp
from jax import lax
from jax.experimental import pallas as pl
from jax.experimental.pallas import tpu as pltpu
from jax.sharding import PartitionSpec as P

HD = 128
SIB_STEPS = 1
HOP_STEPS = 3
CUTS = 1
HEADS_AT_ONCE = 4


def grid_of(ring):
    chips = ring // 2
    short = 1
    while (short * 2) ** 2 <= chips and chips % (short * 2) == 0:
        short *= 2
    return chips // short, short


def kernel(
    ring, heads, kv_heads,
    q_hbm, nk_ref, nv_ref, pk_ref, pv_ref, poolk_ref, poolv_ref, owners_ref, lengths_ref,
    out_hbm,
    x, sib_s, sib_r, in_up, in_dn, up_s, up_r, dn_s, dn_r, kvf, bias, q_ref, out_ref,
    send_sems, recv_sems, q_sem, out_sems,
):
    long, short = grid_of(ring)
    me = lax.axis_index("ctx")
    core = lax.rem(me, 2)
    chip = lax.div(me, 2)
    py = lax.rem(chip, short)
    pz = lax.div(chip, short)
    sibling = me + 1 - 2 * core
    pieces = poolk_ref.shape[1] * CUTS
    blk = poolk_ref.shape[2] // CUTS
    chunks = kv_heads * pieces
    own_rows = pk_ref.shape[0]
    pre = own_rows * ring // pieces
    rows = q_hbm.shape[0]
    group = heads // kv_heads

    q_copy = pltpu.make_async_copy(q_hbm, q_ref, q_sem)
    q_copy.start()
    barrier = pltpu.get_barrier_semaphore()

    def greet(target):
        pl.semaphore_signal(barrier, inc=1, device_id={"ctx": target})

    greet(sibling)
    for pos, size, step in ((py, short, 2), (pz, long, 2 * short)):
        @pl.when(pos > 0)
        def _():
            greet(me - step)

        @pl.when(pos < size - 1)
        def _():
            greet(me + step)

    peers = 1
    for pos, size in ((py, short), (pz, long)):
        peers = peers + jnp.where(pos > 0, 1, 0) + jnp.where(pos < size - 1, 1, 0)
    pl.semaphore_wait(barrier, peers)

    def remote(kind, i, src, dst, target):
        return pltpu.make_async_remote_copy(
            src_ref=src, dst_ref=dst, send_sem=send_sems.at[kind, i], recv_sem=recv_sems.at[kind, i],
            device_id={"ctx": target}, device_id_type=pl.DeviceIdType.MESH,
        )

    length = lengths_ref[0]
    tok = lax.broadcasted_iota(jnp.int32, (rows, rows), 0)
    key = lax.broadcasted_iota(jnp.int32, (rows, rows), 1)
    bias[...] = jnp.where((key <= tok) & (key < length), 0.0, -1e30)

    def cols(g):
        return pl.ds(pl.multiple_of(g * HD, HD), HD)

    def build(i):
        g, b = lax.div(i, pieces), lax.rem(i, pieces)
        page_of = lax.div(b, CUTS)
        start = pl.multiple_of(lax.rem(b, CUTS) * blk, blk)
        mine = jnp.where(owners_ref[page_of] == me, 1.0, 0.0).astype(jnp.float32)
        row = lax.broadcasted_iota(jnp.int32, (pre, HD), 0) + b * pre
        in_mine = (row >= me * own_rows) & (row < (me + 1) * own_rows)
        parts = []
        for pool, pre_ref in ((poolk_ref, pk_ref), (poolv_ref, pv_ref)):
            page = pool[0, page_of, pl.ds(start, blk), cols(g)]
            page = page * jnp.full(page.shape, mine, jnp.float32).astype(jnp.bfloat16)
            mine_pre = pre_ref[:, cols(g)].astype(jnp.float32)
            tiled = jnp.concatenate([mine_pre] * (pre // own_rows), axis=0)
            parts.append((page, jnp.where(in_mine, tiled, 0.0).astype(jnp.bfloat16)))
        is_k = core == 0

        @pl.when(is_k)
        def _():
            x[i, :blk], x[i, blk:] = parts[0]
            sib_s[i, :blk], sib_s[i, blk:] = parts[1]

        @pl.when(jnp.logical_not(is_k))
        def _():
            x[i, :blk], x[i, blk:] = parts[1]
            sib_s[i, :blk], sib_s[i, blk:] = parts[0]

    def valid(i):
        return (i >= 0) & (i < chunks)

    first_is_y = core == 0

    def pick(if_y, if_z):
        return jnp.where(first_is_y, if_y, if_z)

    p1, l1, s1 = pick(py, pz), pick(short, long), pick(2, 2 * short)
    p2, l2, s2 = pick(pz, py), pick(long, short), pick(2 * short, 2)
    depth = lax.div(l1, 2)
    even = 1 - lax.rem(l1, 2)
    r_base = SIB_STEPS
    s_base = r_base + depth * HOP_STEPS
    b_base = s_base + (l2 - 1) * HOP_STEPS

    def root(i):
        return depth - lax.rem(i, 2) * even

    def in_up_copy(i):
        return remote(1, i, x.at[i], in_up.at[i], me + s1)

    def in_dn_copy(i):
        return remote(2, i, x.at[i], in_dn.at[i], me - s1)

    def up_copy(i):
        return remote(3, i, up_s.at[i], up_r.at[i], me + s2)

    def dn_copy(i):
        return remote(4, i, dn_s.at[i], dn_r.at[i], me - s2)

    def share_copy(i):
        return remote(5, i, kvf.at[core, i], kvf.at[core, i], sibling)

    def out_up_copy(i):
        return remote(6, i, kvf.at[core, i], kvf.at[core, i], me + s1)

    def out_dn_copy(i):
        return remote(7, i, kvf.at[core, i], kvf.at[core, i], me - s1)

    def gather_in(t):
        iu = t - r_base - p1 * HOP_STEPS

        @pl.when(valid(iu))
        def _():
            @pl.when(p1 < root(iu))
            def _():
                @pl.when(p1 > 0)
                def _():
                    in_up_copy(iu).wait_recv()
                    x[iu] = x[iu] + in_up[iu]

                in_up_copy(iu).start()

        dn = t - r_base - (l1 - 1 - p1) * HOP_STEPS

        @pl.when(valid(dn))
        def _():
            @pl.when(p1 > root(dn))
            def _():
                @pl.when(p1 < l1 - 1)
                def _():
                    in_dn_copy(dn).wait_recv()
                    x[dn] = x[dn] + in_dn[dn]

                in_dn_copy(dn).start()

        ir = t - s_base

        @pl.when(valid(ir))
        def _():
            @pl.when(p1 == root(ir))
            def _():
                @pl.when(p1 > 0)
                def _():
                    in_up_copy(ir).wait_recv()
                    x[ir] = x[ir] + in_up[ir]

                @pl.when(p1 < l1 - 1)
                def _():
                    in_dn_copy(ir).wait_recv()
                    x[ir] = x[ir] + in_dn[ir]

    def across(t):
        up = t - s_base - p2 * HOP_STEPS

        @pl.when(valid(up))
        def _():
            @pl.when(p1 == root(up))
            def _():
                @pl.when(p2 > 0)
                def _():
                    up_copy(up).wait_recv()

                @pl.when(p2 < l2 - 1)
                def _():
                    @pl.when(p2 > 0)
                    def _():
                        up_s[up] = x[up] + up_r[up]

                    @pl.when(p2 == 0)
                    def _():
                        up_s[up] = x[up]

                    up_copy(up).start()

        dn = t - s_base - (l2 - 1 - p2) * HOP_STEPS

        @pl.when(valid(dn))
        def _():
            @pl.when(p1 == root(dn))
            def _():
                @pl.when(p2 < l2 - 1)
                def _():
                    dn_copy(dn).wait_recv()

                @pl.when(p2 > 0)
                def _():
                    @pl.when(p2 < l2 - 1)
                    def _():
                        dn_s[dn] = x[dn] + dn_r[dn]

                    @pl.when(p2 == l2 - 1)
                    def _():
                        dn_s[dn] = x[dn]

                    dn_copy(dn).start()

    def spread(t):
        end = t - b_base

        @pl.when(valid(end))
        def _():
            @pl.when(p1 == root(end))
            def _():
                @pl.when((p2 > 0) & (p2 < l2 - 1))
                def _():
                    kvf[core, end] = x[end] + up_r[end] + dn_r[end]

                @pl.when((p2 > 0) & (p2 == l2 - 1))
                def _():
                    kvf[core, end] = x[end] + up_r[end]

                @pl.when((p2 == 0) & (p2 < l2 - 1))
                def _():
                    kvf[core, end] = x[end] + dn_r[end]

                @pl.when(l2 == 1)
                def _():
                    kvf[core, end] = x[end]

                @pl.when(p1 < l1 - 1)
                def _():
                    out_up_copy(end).start()

                @pl.when(p1 > 0)
                def _():
                    out_dn_copy(end).start()

                share_copy(end).start()

        for back in (0, 1):
            above = p1 - (depth - back)
            i = t - b_base - jnp.where(above > 0, above, -above) * HOP_STEPS

            @pl.when(valid(i) & (above != 0))
            def _():
                @pl.when(root(i) == depth - back)
                def _():
                    @pl.when(above > 0)
                    def _():
                        out_up_copy(i).wait_recv()

                        @pl.when(p1 < l1 - 1)
                        def _():
                            out_up_copy(i).start()

                    @pl.when(above < 0)
                    def _():
                        out_dn_copy(i).wait_recv()

                        @pl.when(p1 > 0)
                        def _():
                            out_dn_copy(i).start()

                    share_copy(i).start()

    live = lax.broadcasted_iota(jnp.int32, (rows, HD), 0) < length
    batches = group // HEADS_AT_ONCE
    score_scale = 1.4426950408889634 / HD**0.5
    wide = HEADS_AT_ONCE * HD

    def result_copy(m):
        columns = pl.ds(pl.multiple_of(m * wide, wide), wide)
        return pltpu.make_async_copy(out_ref.at[:, columns], out_hbm.at[:, columns], out_sems.at[m])

    all_rows = pieces * (blk + pre)

    def attend(m):
        g, part = lax.div(m, batches), lax.rem(m, batches)
        first = g * group + part * HEADS_AT_ONCE
        q = jnp.concatenate([q_ref[:, cols(first + j)] for j in range(HEADS_AT_ONCE)], axis=0)
        keys = kvf[0, pl.ds(g * pieces, pieces)].reshape(all_rows, HD)
        values = kvf[1, pl.ds(g * pieces, pieces)].reshape(all_rows, HD)
        dims = (((1,), (1,)), ((), ()))
        s_far = lax.dot_general(q, keys, dims, preferred_element_type=jnp.float32)
        s_own = lax.dot_general(q, nk_ref[:, cols(g)], dims, preferred_element_type=jnp.float32)
        s_own = s_own + jnp.concatenate([bias[...]] * HEADS_AT_ONCE, axis=0)
        top = jnp.maximum(jnp.max(s_far, axis=1, keepdims=True), jnp.max(s_own, axis=1, keepdims=True))
        w_far = jnp.exp2((s_far - top) * score_scale).astype(jnp.bfloat16)
        w_own = jnp.exp2((s_own - top) * score_scale).astype(jnp.bfloat16)
        v_far = jnp.concatenate([values, jnp.ones_like(values)], axis=1)
        own = nv_ref[:, cols(g)]
        v_own = jnp.concatenate([own, jnp.ones_like(own)], axis=1)
        summed = jnp.dot(w_far, v_far, preferred_element_type=jnp.float32)
        summed += jnp.dot(w_own, v_own, preferred_element_type=jnp.float32)
        result = summed[:, :HD] / summed[:, HD:]
        for j in range(HEADS_AT_ONCE):
            piece = jnp.where(live, result[j * rows : (j + 1) * rows], 0.0)
            out_ref[:, cols(first + j)] = piece.astype(out_ref.dtype)

    hops = max(2 * (short // 2) + long - 1, 2 * (long // 2) + short - 1)
    c_base = SIB_STEPS + hops * HOP_STEPS + SIB_STEPS
    attends = kv_heads * batches
    per = max(pieces // batches, 1)
    steps = c_base + max(chunks, pieces + (attends - 1) * per)

    def one_step(t, carry):
        @pl.when(t < chunks)
        def _():
            build(t)
            remote(0, t, sib_s.at[t], sib_r.at[t], sibling).start()

        i = t - r_base

        @pl.when(valid(i))
        def _():
            remote(0, i, sib_s.at[i], sib_r.at[i], sibling).wait_recv()
            x[i] = x[i] + sib_r[i]

        gather_in(t)
        across(t)
        spread(t)
        i_c = t - c_base

        @pl.when(valid(i_c))
        def _():
            remote(5, i_c, kvf.at[core, i_c], kvf.at[1 - core, i_c], sibling).wait_recv()

        late = t - c_base - (pieces - 1)

        @pl.when(late == 0)
        def _():
            q_copy.wait()

        @pl.when((late >= 0) & (late < attends * per) & (lax.rem(late, per) == 0))
        def _():
            m = lax.div(late, per)
            attend(m)
            result_copy(m).start()

        return carry

    lax.fori_loop(0, steps, one_step, 0)

    def drain(i, carry):
        remote(0, i, sib_s.at[i], sib_r.at[i], sibling).wait_send()
        share_copy(i).wait_send()
        at = root(i)
        for used, copy in (
            (p1 < at, in_up_copy),
            (p1 > at, in_dn_copy),
            ((p1 == at) & (p2 < l2 - 1), up_copy),
            ((p1 == at) & (p2 > 0), dn_copy),
            ((p1 >= at) & (p1 < l1 - 1), out_up_copy),
            ((p1 <= at) & (p1 > 0), out_dn_copy),
        ):
            @pl.when(used)
            def _():
                copy(i).wait_send()

        return carry

    lax.fori_loop(0, chunks, drain, 0)

    def drain_result(m, carry):
        result_copy(m).wait()
        return carry

    lax.fori_loop(0, attends, drain_result, 0)


def solution(mesh):
    ring = mesh.shape["ctx"]

    def body(queries, new_keys, new_values, prefix_keys, prefix_values, pool_keys, pool_values, owners, lengths):
        heads = queries.shape[1] // HD
        kv_heads = new_keys.shape[1] // HD
        pieces = pool_keys.shape[1] * CUTS
        chunks = kv_heads * pieces
        c_rows = pool_keys.shape[2] // CUTS + prefix_keys.shape[0] * ring // pieces
        chunk_buf = pltpu.VMEM((chunks, c_rows, HD), jnp.bfloat16)
        vm = pl.BlockSpec(memory_space=pltpu.VMEM)
        hbm = pl.BlockSpec(memory_space=pl.ANY)
        sm = pl.BlockSpec(memory_space=pltpu.SMEM)
        return pl.pallas_call(
            functools.partial(kernel, ring, heads, kv_heads),
            out_shape=jax.ShapeDtypeStruct(queries.shape, jnp.bfloat16),
            in_specs=[hbm] + [vm] * 6 + [sm] * 2,
            out_specs=hbm,
            scratch_shapes=[chunk_buf] * 9
            + [
                pltpu.VMEM((2, chunks, c_rows, HD), jnp.bfloat16),
                pltpu.VMEM((queries.shape[0], queries.shape[0]), jnp.float32),
                pltpu.VMEM(queries.shape, jnp.bfloat16),
                pltpu.VMEM(queries.shape, jnp.bfloat16),
                pltpu.SemaphoreType.DMA((8, chunks)),
                pltpu.SemaphoreType.DMA((8, chunks)),
                pltpu.SemaphoreType.DMA,
                pltpu.SemaphoreType.DMA((heads // HEADS_AT_ONCE,)),
            ],
            compiler_params=pltpu.CompilerParams(
                collective_id=0, has_side_effects=True, vmem_limit_bytes=67043328
            ),
        )(queries, new_keys, new_values, prefix_keys, prefix_values, pool_keys, pool_values, owners, lengths)

    two = P(("groups", "ctx"), None)
    four = P(("groups", "ctx"), None, None, None)
    return jax.shard_map(
        body, mesh=mesh, in_specs=(two,) * 5 + (four,) * 2 + (P("groups"), P(("groups", "ctx"))),
        out_specs=two, check_vma=False,
    )
```

```python
import functools

import jax
import jax.numpy as jnp
from jax import lax
from jax.experimental import pallas as pl
from jax.experimental.pallas import tpu as pltpu
from jax.sharding import PartitionSpec as P

HD = 128
SIB_STEPS = 1
HOP_STEPS = 3
CUTS = 1
HEADS_AT_ONCE = 4
SUB = 2


def grid_of(ring):
    chips = ring // 2
    short = 1
    while (short * 2) ** 2 <= chips and chips % (short * 2) == 0:
        short *= 2
    return chips // short, short


def kernel(
    ring, heads, kv_heads,
    q_hbm, nk_ref, nv_ref, pk_ref, pv_ref, poolk_ref, poolv_ref, owners_ref, lengths_ref,
    out_hbm,
    x, sib_s, sib_r, in_up, in_dn, up_s, up_r, dn_s, dn_r, kvf, bias, q_ref, out_ref,
    send_sems, recv_sems, q_sem, out_sems,
):
    long, short = grid_of(ring)
    me = lax.axis_index("ctx")
    core = lax.rem(me, 2)
    chip = lax.div(me, 2)
    py = lax.rem(chip, short)
    pz = lax.div(chip, short)
    sibling = me + 1 - 2 * core
    pieces = poolk_ref.shape[1] * CUTS
    blk = poolk_ref.shape[2] // CUTS
    chunks = kv_heads * pieces
    own_rows = pk_ref.shape[0]
    pre = own_rows * ring // pieces
    rows = q_hbm.shape[0]
    group = heads // kv_heads

    q_copy = pltpu.make_async_copy(q_hbm, q_ref, q_sem)
    q_copy.start()
    barrier = pltpu.get_barrier_semaphore()

    def greet(target):
        pl.semaphore_signal(barrier, inc=1, device_id={"ctx": target})

    greet(sibling)
    for pos, size, step in ((py, short, 2), (pz, long, 2 * short)):
        @pl.when(pos > 0)
        def _():
            greet(me - step)

        @pl.when(pos < size - 1)
        def _():
            greet(me + step)

    peers = 1
    for pos, size in ((py, short), (pz, long)):
        peers = peers + jnp.where(pos > 0, 1, 0) + jnp.where(pos < size - 1, 1, 0)
    pl.semaphore_wait(barrier, peers)

    def remote(kind, i, src, dst, target):
        return pltpu.make_async_remote_copy(
            src_ref=src, dst_ref=dst, send_sem=send_sems.at[kind, i], recv_sem=recv_sems.at[kind, i],
            device_id={"ctx": target}, device_id_type=pl.DeviceIdType.MESH,
        )

    length = lengths_ref[0]
    tok = lax.broadcasted_iota(jnp.int32, (rows, rows), 0)
    key = lax.broadcasted_iota(jnp.int32, (rows, rows), 1)
    bias[...] = jnp.where((key <= tok) & (key < length), 0.0, -1e30)

    def cols(g):
        return pl.ds(pl.multiple_of(g * HD, HD), HD)

    def build(i):
        g, b = lax.div(i, pieces), lax.rem(i, pieces)
        page_of = lax.div(b, CUTS)
        start = pl.multiple_of(lax.rem(b, CUTS) * blk, blk)
        mine = jnp.where(owners_ref[page_of] == me, 1.0, 0.0).astype(jnp.float32)
        row = lax.broadcasted_iota(jnp.int32, (pre, HD), 0) + b * pre
        in_mine = (row >= me * own_rows) & (row < (me + 1) * own_rows)
        parts = []
        for pool, pre_ref in ((poolk_ref, pk_ref), (poolv_ref, pv_ref)):
            page = pool[0, page_of, pl.ds(start, blk), cols(g)]
            page = page * jnp.full(page.shape, mine, jnp.float32).astype(jnp.bfloat16)
            mine_pre = pre_ref[:, cols(g)].astype(jnp.float32)
            tiled = jnp.concatenate([mine_pre] * (pre // own_rows), axis=0)
            parts.append((page, jnp.where(in_mine, tiled, 0.0).astype(jnp.bfloat16)))
        is_k = core == 0

        @pl.when(is_k)
        def _():
            x[i, :blk], x[i, blk:] = parts[0]
            sib_s[i, :blk], sib_s[i, blk:] = parts[1]

        @pl.when(jnp.logical_not(is_k))
        def _():
            x[i, :blk], x[i, blk:] = parts[1]
            sib_s[i, :blk], sib_s[i, blk:] = parts[0]

    def valid(i):
        return (i >= 0) & (i < chunks)

    first_is_y = core == 0

    def pick(if_y, if_z):
        return jnp.where(first_is_y, if_y, if_z)

    p1, l1, s1 = pick(py, pz), pick(short, long), pick(2, 2 * short)
    p2, l2, s2 = pick(pz, py), pick(long, short), pick(2 * short, 2)
    depth = lax.div(l1, 2)
    even = 1 - lax.rem(l1, 2)
    r_base = SIB_STEPS
    s_base = r_base + depth * HOP_STEPS
    b_base = s_base + (l2 - 1) * HOP_STEPS

    def root(i):
        return depth - lax.rem(i, 2) * even

    def in_up_copy(i):
        return remote(1, i, x.at[i], in_up.at[i], me + s1)

    def in_dn_copy(i):
        return remote(2, i, x.at[i], in_dn.at[i], me - s1)

    def up_copy(i):
        return remote(3, i, up_s.at[i], up_r.at[i], me + s2)

    def dn_copy(i):
        return remote(4, i, dn_s.at[i], dn_r.at[i], me - s2)

    def share_copy(i):
        return remote(5, i, kvf.at[core, i], kvf.at[core, i], sibling)

    def out_up_copy(i):
        return remote(6, i, kvf.at[core, i], kvf.at[core, i], me + s1)

    def out_dn_copy(i):
        return remote(7, i, kvf.at[core, i], kvf.at[core, i], me - s1)

    def gather_in(t):
        iu = t - r_base - p1 * HOP_STEPS

        @pl.when(valid(iu))
        def _():
            @pl.when(p1 < root(iu))
            def _():
                @pl.when(p1 > 0)
                def _():
                    in_up_copy(iu).wait_recv()
                    x[iu] = x[iu] + in_up[iu]

                in_up_copy(iu).start()

        dn = t - r_base - (l1 - 1 - p1) * HOP_STEPS

        @pl.when(valid(dn))
        def _():
            @pl.when(p1 > root(dn))
            def _():
                @pl.when(p1 < l1 - 1)
                def _():
                    in_dn_copy(dn).wait_recv()
                    x[dn] = x[dn] + in_dn[dn]

                in_dn_copy(dn).start()

        ir = t - s_base

        @pl.when(valid(ir))
        def _():
            @pl.when(p1 == root(ir))
            def _():
                @pl.when(p1 > 0)
                def _():
                    in_up_copy(ir).wait_recv()
                    x[ir] = x[ir] + in_up[ir]

                @pl.when(p1 < l1 - 1)
                def _():
                    in_dn_copy(ir).wait_recv()
                    x[ir] = x[ir] + in_dn[ir]

    def across(t):
        up = t - s_base - p2 * HOP_STEPS

        @pl.when(valid(up))
        def _():
            @pl.when(p1 == root(up))
            def _():
                @pl.when(p2 > 0)
                def _():
                    up_copy(up).wait_recv()

                @pl.when(p2 < l2 - 1)
                def _():
                    @pl.when(p2 > 0)
                    def _():
                        up_s[up] = x[up] + up_r[up]

                    @pl.when(p2 == 0)
                    def _():
                        up_s[up] = x[up]

                    up_copy(up).start()

        dn = t - s_base - (l2 - 1 - p2) * HOP_STEPS

        @pl.when(valid(dn))
        def _():
            @pl.when(p1 == root(dn))
            def _():
                @pl.when(p2 < l2 - 1)
                def _():
                    dn_copy(dn).wait_recv()

                @pl.when(p2 > 0)
                def _():
                    @pl.when(p2 < l2 - 1)
                    def _():
                        dn_s[dn] = x[dn] + dn_r[dn]

                    @pl.when(p2 == l2 - 1)
                    def _():
                        dn_s[dn] = x[dn]

                    dn_copy(dn).start()

    def spread(t):
        end = t - b_base

        @pl.when(valid(end))
        def _():
            @pl.when(p1 == root(end))
            def _():
                @pl.when((p2 > 0) & (p2 < l2 - 1))
                def _():
                    kvf[core, end] = x[end] + up_r[end] + dn_r[end]

                @pl.when((p2 > 0) & (p2 == l2 - 1))
                def _():
                    kvf[core, end] = x[end] + up_r[end]

                @pl.when((p2 == 0) & (p2 < l2 - 1))
                def _():
                    kvf[core, end] = x[end] + dn_r[end]

                @pl.when(l2 == 1)
                def _():
                    kvf[core, end] = x[end]

                @pl.when(p1 < l1 - 1)
                def _():
                    out_up_copy(end).start()

                @pl.when(p1 > 0)
                def _():
                    out_dn_copy(end).start()

                share_copy(end).start()

        for back in (0, 1):
            above = p1 - (depth - back)
            i = t - b_base - jnp.where(above > 0, above, -above) * HOP_STEPS

            @pl.when(valid(i) & (above != 0))
            def _():
                @pl.when(root(i) == depth - back)
                def _():
                    @pl.when(above > 0)
                    def _():
                        out_up_copy(i).wait_recv()

                        @pl.when(p1 < l1 - 1)
                        def _():
                            out_up_copy(i).start()

                    @pl.when(above < 0)
                    def _():
                        out_dn_copy(i).wait_recv()

                        @pl.when(p1 > 0)
                        def _():
                            out_dn_copy(i).start()

                    share_copy(i).start()

    live = lax.broadcasted_iota(jnp.int32, (rows, HD), 0) < length
    batches = group // HEADS_AT_ONCE
    score_scale = 1.4426950408889634 / HD**0.5
    wide = HEADS_AT_ONCE * HD

    def result_copy(m):
        columns = pl.ds(pl.multiple_of(m * wide, wide), wide)
        return pltpu.make_async_copy(out_ref.at[:, columns], out_hbm.at[:, columns], out_sems.at[m])

    all_rows = pieces * (blk + pre)

    def attend(m):
        g, part = lax.div(m, batches), lax.rem(m, batches)
        first = g * group + part * HEADS_AT_ONCE
        keys = kvf[0, pl.ds(g * pieces, pieces)].reshape(all_rows, HD)
        values = kvf[1, pl.ds(g * pieces, pieces)].reshape(all_rows, HD)
        dims = (((1,), (1,)), ((), ()))
        v_far = jnp.concatenate([values, jnp.ones_like(values)], axis=1)
        own_k, own_v = nk_ref[:, cols(g)], nv_ref[:, cols(g)]
        v_own = jnp.concatenate([own_v, jnp.ones_like(own_v)], axis=1)
        mask = jnp.concatenate([bias[...]] * SUB, axis=0)
        for sub in range(0, HEADS_AT_ONCE, SUB):
            q = jnp.concatenate([q_ref[:, cols(first + sub + j)] for j in range(SUB)], axis=0)
            s_far = lax.dot_general(q, keys, dims, preferred_element_type=jnp.float32)
            s_own = lax.dot_general(q, own_k, dims, preferred_element_type=jnp.float32) + mask
            top = jnp.maximum(jnp.max(s_far, axis=1, keepdims=True), jnp.max(s_own, axis=1, keepdims=True))
            w_far = jnp.exp2((s_far - top) * score_scale).astype(jnp.bfloat16)
            w_own = jnp.exp2((s_own - top) * score_scale).astype(jnp.bfloat16)
            summed = jnp.dot(w_far, v_far, preferred_element_type=jnp.float32)
            summed += jnp.dot(w_own, v_own, preferred_element_type=jnp.float32)
            result = summed[:, :HD] / summed[:, HD:]
            for j in range(SUB):
                piece = jnp.where(live, result[j * rows : (j + 1) * rows], 0.0)
                out_ref[:, cols(first + sub + j)] = piece.astype(out_ref.dtype)

    hops = max(2 * (short // 2) + long - 1, 2 * (long // 2) + short - 1)
    c_base = SIB_STEPS + hops * HOP_STEPS + SIB_STEPS
    attends = kv_heads * batches
    per = max(pieces // batches, 1)
    steps = c_base + max(chunks, pieces + (attends - 1) * per)

    def one_step(t, carry):
        @pl.when(t < chunks)
        def _():
            build(t)
            remote(0, t, sib_s.at[t], sib_r.at[t], sibling).start()

        i = t - r_base

        @pl.when(valid(i))
        def _():
            remote(0, i, sib_s.at[i], sib_r.at[i], sibling).wait_recv()
            x[i] = x[i] + sib_r[i]

        gather_in(t)
        across(t)
        spread(t)
        i_c = t - c_base

        @pl.when(valid(i_c))
        def _():
            remote(5, i_c, kvf.at[core, i_c], kvf.at[1 - core, i_c], sibling).wait_recv()

        late = t - c_base - (pieces - 1)

        @pl.when(late == 0)
        def _():
            q_copy.wait()

        @pl.when((late >= 0) & (late < attends * per) & (lax.rem(late, per) == 0))
        def _():
            m = lax.div(late, per)
            attend(m)
            result_copy(m).start()

        return carry

    lax.fori_loop(0, steps, one_step, 0)

    def drain(i, carry):
        remote(0, i, sib_s.at[i], sib_r.at[i], sibling).wait_send()
        share_copy(i).wait_send()
        at = root(i)
        for used, copy in (
            (p1 < at, in_up_copy),
            (p1 > at, in_dn_copy),
            ((p1 == at) & (p2 < l2 - 1), up_copy),
            ((p1 == at) & (p2 > 0), dn_copy),
            ((p1 >= at) & (p1 < l1 - 1), out_up_copy),
            ((p1 <= at) & (p1 > 0), out_dn_copy),
        ):
            @pl.when(used)
            def _():
                copy(i).wait_send()

        return carry

    lax.fori_loop(0, chunks, drain, 0)

    def drain_result(m, carry):
        result_copy(m).wait()
        return carry

    lax.fori_loop(0, attends, drain_result, 0)


def solution(mesh):
    ring = mesh.shape["ctx"]

    def body(queries, new_keys, new_values, prefix_keys, prefix_values, pool_keys, pool_values, owners, lengths):
        heads = queries.shape[1] // HD
        kv_heads = new_keys.shape[1] // HD
        pieces = pool_keys.shape[1] * CUTS
        chunks = kv_heads * pieces
        c_rows = pool_keys.shape[2] // CUTS + prefix_keys.shape[0] * ring // pieces
        chunk_buf = pltpu.VMEM((chunks, c_rows, HD), jnp.bfloat16)
        vm = pl.BlockSpec(memory_space=pltpu.VMEM)
        hbm = pl.BlockSpec(memory_space=pl.ANY)
        sm = pl.BlockSpec(memory_space=pltpu.SMEM)
        return pl.pallas_call(
            functools.partial(kernel, ring, heads, kv_heads),
            out_shape=jax.ShapeDtypeStruct(queries.shape, jnp.bfloat16),
            in_specs=[hbm] + [vm] * 6 + [sm] * 2,
            out_specs=hbm,
            scratch_shapes=[chunk_buf] * 9
            + [
                pltpu.VMEM((2, chunks, c_rows, HD), jnp.bfloat16),
                pltpu.VMEM((queries.shape[0], queries.shape[0]), jnp.float32),
                pltpu.VMEM(queries.shape, jnp.bfloat16),
                pltpu.VMEM(queries.shape, jnp.bfloat16),
                pltpu.SemaphoreType.DMA((8, chunks)),
                pltpu.SemaphoreType.DMA((8, chunks)),
                pltpu.SemaphoreType.DMA,
                pltpu.SemaphoreType.DMA((heads // HEADS_AT_ONCE,)),
            ],
            compiler_params=pltpu.CompilerParams(
                collective_id=0, has_side_effects=True, vmem_limit_bytes=67043328
            ),
        )(queries, new_keys, new_values, prefix_keys, prefix_values, pool_keys, pool_values, owners, lengths)

    two = P(("groups", "ctx"), None)
    four = P(("groups", "ctx"), None, None, None)
    return jax.shard_map(
        body, mesh=mesh, in_specs=(two,) * 5 + (four,) * 2 + (P("groups"), P(("groups", "ctx"))),
        out_specs=two, check_vma=False,
    )
```

```python
import functools

import jax
import jax.numpy as jnp
from jax import lax
from jax.experimental import pallas as pl
from jax.experimental.pallas import tpu as pltpu
from jax.sharding import PartitionSpec as P

HD = 128
SIB_STEPS = 1
HOP_STEPS = 3
CUTS = 1
HEADS_AT_ONCE = 4
SUB = 2


def grid_of(ring):
    chips = ring // 2
    short = 1
    while (short * 2) ** 2 <= chips and chips % (short * 2) == 0:
        short *= 2
    return chips // short, short


def kernel(
    ring, heads, kv_heads,
    q_hbm, nk_ref, nv_ref, pk_ref, pv_ref, poolk_hbm, poolv_hbm, owners_ref, lengths_ref,
    out_hbm,
    x, sib_s, sib_r, in_up, in_dn, up_s, up_r, dn_s, dn_r, kvf, bias, q_ref, out_ref, poolk_ref, poolv_ref,
    send_sems, recv_sems, q_sem, out_sems, pool_sems,
):
    long, short = grid_of(ring)
    me = lax.axis_index("ctx")
    core = lax.rem(me, 2)
    chip = lax.div(me, 2)
    py = lax.rem(chip, short)
    pz = lax.div(chip, short)
    sibling = me + 1 - 2 * core
    pieces = poolk_ref.shape[1] * CUTS
    blk = poolk_ref.shape[2] // CUTS
    chunks = kv_heads * pieces
    own_rows = pk_ref.shape[0]
    pre = own_rows * ring // pieces
    rows = q_hbm.shape[0]
    group = heads // kv_heads

    q_copy = pltpu.make_async_copy(q_hbm, q_ref, q_sem)
    pool_copies = [
        pltpu.make_async_copy(poolk_hbm, poolk_ref, pool_sems.at[0]),
        pltpu.make_async_copy(poolv_hbm, poolv_ref, pool_sems.at[1]),
    ]
    for copy in pool_copies:
        copy.start()
    q_copy.start()
    barrier = pltpu.get_barrier_semaphore()

    def greet(target):
        pl.semaphore_signal(barrier, inc=1, device_id={"ctx": target})

    greet(sibling)
    for pos, size, step in ((py, short, 2), (pz, long, 2 * short)):
        @pl.when(pos > 0)
        def _():
            greet(me - step)

        @pl.when(pos < size - 1)
        def _():
            greet(me + step)

    peers = 1
    for pos, size in ((py, short), (pz, long)):
        peers = peers + jnp.where(pos > 0, 1, 0) + jnp.where(pos < size - 1, 1, 0)
    pl.semaphore_wait(barrier, peers)

    def remote(kind, i, src, dst, target):
        return pltpu.make_async_remote_copy(
            src_ref=src, dst_ref=dst, send_sem=send_sems.at[kind, i], recv_sem=recv_sems.at[kind, i],
            device_id={"ctx": target}, device_id_type=pl.DeviceIdType.MESH,
        )

    length = lengths_ref[0]
    tok = lax.broadcasted_iota(jnp.int32, (rows, rows), 0)
    key = lax.broadcasted_iota(jnp.int32, (rows, rows), 1)
    bias[...] = jnp.where((key <= tok) & (key < length), 0.0, -1e30)

    def cols(g):
        return pl.ds(pl.multiple_of(g * HD, HD), HD)

    def build(i):
        g, b = lax.div(i, pieces), lax.rem(i, pieces)
        page_of = lax.div(b, CUTS)
        start = pl.multiple_of(lax.rem(b, CUTS) * blk, blk)
        mine = jnp.where(owners_ref[page_of] == me, 1.0, 0.0).astype(jnp.float32)
        row = lax.broadcasted_iota(jnp.int32, (pre, HD), 0) + b * pre
        in_mine = (row >= me * own_rows) & (row < (me + 1) * own_rows)
        parts = []
        for pool, pre_ref in ((poolk_ref, pk_ref), (poolv_ref, pv_ref)):
            page = pool[0, page_of, pl.ds(start, blk), cols(g)]
            page = page * jnp.full(page.shape, mine, jnp.float32).astype(jnp.bfloat16)
            mine_pre = pre_ref[:, cols(g)].astype(jnp.float32)
            tiled = jnp.concatenate([mine_pre] * (pre // own_rows), axis=0)
            parts.append((page, jnp.where(in_mine, tiled, 0.0).astype(jnp.bfloat16)))
        is_k = core == 0

        @pl.when(is_k)
        def _():
            x[i, :blk], x[i, blk:] = parts[0]
            sib_s[i, :blk], sib_s[i, blk:] = parts[1]

        @pl.when(jnp.logical_not(is_k))
        def _():
            x[i, :blk], x[i, blk:] = parts[1]
            sib_s[i, :blk], sib_s[i, blk:] = parts[0]

    def valid(i):
        return (i >= 0) & (i < chunks)

    first_is_y = core == 0

    def pick(if_y, if_z):
        return jnp.where(first_is_y, if_y, if_z)

    p1, l1, s1 = pick(py, pz), pick(short, long), pick(2, 2 * short)
    p2, l2, s2 = pick(pz, py), pick(long, short), pick(2 * short, 2)
    depth = lax.div(l1, 2)
    even = 1 - lax.rem(l1, 2)
    r_base = SIB_STEPS
    s_base = r_base + depth * HOP_STEPS
    b_base = s_base + (l2 - 1) * HOP_STEPS

    def root(i):
        return depth - lax.rem(i, 2) * even

    def in_up_copy(i):
        return remote(1, i, x.at[i], in_up.at[i], me + s1)

    def in_dn_copy(i):
        return remote(2, i, x.at[i], in_dn.at[i], me - s1)

    def up_copy(i):
        return remote(3, i, up_s.at[i], up_r.at[i], me + s2)

    def dn_copy(i):
        return remote(4, i, dn_s.at[i], dn_r.at[i], me - s2)

    def share_copy(i):
        return remote(5, i, kvf.at[core, i], kvf.at[core, i], sibling)

    def out_up_copy(i):
        return remote(6, i, kvf.at[core, i], kvf.at[core, i], me + s1)

    def out_dn_copy(i):
        return remote(7, i, kvf.at[core, i], kvf.at[core, i], me - s1)

    def gather_in(t):
        iu = t - r_base - p1 * HOP_STEPS

        @pl.when(valid(iu))
        def _():
            @pl.when(p1 < root(iu))
            def _():
                @pl.when(p1 > 0)
                def _():
                    in_up_copy(iu).wait_recv()
                    x[iu] = x[iu] + in_up[iu]

                in_up_copy(iu).start()

        dn = t - r_base - (l1 - 1 - p1) * HOP_STEPS

        @pl.when(valid(dn))
        def _():
            @pl.when(p1 > root(dn))
            def _():
                @pl.when(p1 < l1 - 1)
                def _():
                    in_dn_copy(dn).wait_recv()
                    x[dn] = x[dn] + in_dn[dn]

                in_dn_copy(dn).start()

        ir = t - s_base

        @pl.when(valid(ir))
        def _():
            @pl.when(p1 == root(ir))
            def _():
                @pl.when(p1 > 0)
                def _():
                    in_up_copy(ir).wait_recv()
                    x[ir] = x[ir] + in_up[ir]

                @pl.when(p1 < l1 - 1)
                def _():
                    in_dn_copy(ir).wait_recv()
                    x[ir] = x[ir] + in_dn[ir]

    def across(t):
        up = t - s_base - p2 * HOP_STEPS

        @pl.when(valid(up))
        def _():
            @pl.when(p1 == root(up))
            def _():
                @pl.when(p2 > 0)
                def _():
                    up_copy(up).wait_recv()

                @pl.when(p2 < l2 - 1)
                def _():
                    @pl.when(p2 > 0)
                    def _():
                        up_s[up] = x[up] + up_r[up]

                    @pl.when(p2 == 0)
                    def _():
                        up_s[up] = x[up]

                    up_copy(up).start()

        dn = t - s_base - (l2 - 1 - p2) * HOP_STEPS

        @pl.when(valid(dn))
        def _():
            @pl.when(p1 == root(dn))
            def _():
                @pl.when(p2 < l2 - 1)
                def _():
                    dn_copy(dn).wait_recv()

                @pl.when(p2 > 0)
                def _():
                    @pl.when(p2 < l2 - 1)
                    def _():
                        dn_s[dn] = x[dn] + dn_r[dn]

                    @pl.when(p2 == l2 - 1)
                    def _():
                        dn_s[dn] = x[dn]

                    dn_copy(dn).start()

    def spread(t):
        end = t - b_base

        @pl.when(valid(end))
        def _():
            @pl.when(p1 == root(end))
            def _():
                @pl.when((p2 > 0) & (p2 < l2 - 1))
                def _():
                    kvf[core, end] = x[end] + up_r[end] + dn_r[end]

                @pl.when((p2 > 0) & (p2 == l2 - 1))
                def _():
                    kvf[core, end] = x[end] + up_r[end]

                @pl.when((p2 == 0) & (p2 < l2 - 1))
                def _():
                    kvf[core, end] = x[end] + dn_r[end]

                @pl.when(l2 == 1)
                def _():
                    kvf[core, end] = x[end]

                @pl.when(p1 < l1 - 1)
                def _():
                    out_up_copy(end).start()

                @pl.when(p1 > 0)
                def _():
                    out_dn_copy(end).start()

                share_copy(end).start()

        for back in (0, 1):
            above = p1 - (depth - back)
            i = t - b_base - jnp.where(above > 0, above, -above) * HOP_STEPS

            @pl.when(valid(i) & (above != 0))
            def _():
                @pl.when(root(i) == depth - back)
                def _():
                    @pl.when(above > 0)
                    def _():
                        out_up_copy(i).wait_recv()

                        @pl.when(p1 < l1 - 1)
                        def _():
                            out_up_copy(i).start()

                    @pl.when(above < 0)
                    def _():
                        out_dn_copy(i).wait_recv()

                        @pl.when(p1 > 0)
                        def _():
                            out_dn_copy(i).start()

                    share_copy(i).start()

    live = lax.broadcasted_iota(jnp.int32, (rows, HD), 0) < length
    batches = group // HEADS_AT_ONCE
    score_scale = 1.4426950408889634 / HD**0.5
    wide = HEADS_AT_ONCE * HD

    def result_copy(m):
        columns = pl.ds(pl.multiple_of(m * wide, wide), wide)
        return pltpu.make_async_copy(out_ref.at[:, columns], out_hbm.at[:, columns], out_sems.at[m])

    all_rows = pieces * (blk + pre)

    def attend(m):
        g, part = lax.div(m, batches), lax.rem(m, batches)
        first = g * group + part * HEADS_AT_ONCE
        keys = kvf[0, pl.ds(g * pieces, pieces)].reshape(all_rows, HD)
        values = kvf[1, pl.ds(g * pieces, pieces)].reshape(all_rows, HD)
        dims = (((1,), (1,)), ((), ()))
        v_far = jnp.concatenate([values, jnp.ones_like(values)], axis=1)
        own_k, own_v = nk_ref[:, cols(g)], nv_ref[:, cols(g)]
        v_own = jnp.concatenate([own_v, jnp.ones_like(own_v)], axis=1)
        mask = jnp.concatenate([bias[...]] * SUB, axis=0)
        for sub in range(0, HEADS_AT_ONCE, SUB):
            q = jnp.concatenate([q_ref[:, cols(first + sub + j)] for j in range(SUB)], axis=0)
            s_far = lax.dot_general(q, keys, dims, preferred_element_type=jnp.float32)
            s_own = lax.dot_general(q, own_k, dims, preferred_element_type=jnp.float32) + mask
            top = jnp.maximum(jnp.max(s_far, axis=1, keepdims=True), jnp.max(s_own, axis=1, keepdims=True))
            w_far = jnp.exp2((s_far - top) * score_scale).astype(jnp.bfloat16)
            w_own = jnp.exp2((s_own - top) * score_scale).astype(jnp.bfloat16)
            summed = jnp.dot(w_far, v_far, preferred_element_type=jnp.float32)
            summed += jnp.dot(w_own, v_own, preferred_element_type=jnp.float32)
            result = summed[:, :HD] / summed[:, HD:]
            for j in range(SUB):
                piece = jnp.where(live, result[j * rows : (j + 1) * rows], 0.0)
                out_ref[:, cols(first + sub + j)] = piece.astype(out_ref.dtype)

    hops = max(2 * (short // 2) + long - 1, 2 * (long // 2) + short - 1)
    c_base = SIB_STEPS + hops * HOP_STEPS + SIB_STEPS
    attends = kv_heads * batches
    per = max(pieces // batches, 1)
    steps = c_base + max(chunks, pieces + (attends - 1) * per)

    def one_step(t, carry):
        @pl.when(t < chunks)
        def _():
            build(t)
            remote(0, t, sib_s.at[t], sib_r.at[t], sibling).start()

        i = t - r_base

        @pl.when(valid(i))
        def _():
            remote(0, i, sib_s.at[i], sib_r.at[i], sibling).wait_recv()
            x[i] = x[i] + sib_r[i]

        gather_in(t)
        across(t)
        spread(t)
        i_c = t - c_base

        @pl.when(valid(i_c))
        def _():
            remote(5, i_c, kvf.at[core, i_c], kvf.at[1 - core, i_c], sibling).wait_recv()

        late = t - c_base - (pieces - 1)

        @pl.when(late == 0)
        def _():
            q_copy.wait()

        @pl.when((late >= 0) & (late < attends * per) & (lax.rem(late, per) == 0))
        def _():
            m = lax.div(late, per)
            attend(m)
            result_copy(m).start()

        return carry

    for copy in pool_copies:
        copy.wait()
    lax.fori_loop(0, steps, one_step, 0)

    def drain(i, carry):
        remote(0, i, sib_s.at[i], sib_r.at[i], sibling).wait_send()
        share_copy(i).wait_send()
        at = root(i)
        for used, copy in (
            (p1 < at, in_up_copy),
            (p1 > at, in_dn_copy),
            ((p1 == at) & (p2 < l2 - 1), up_copy),
            ((p1 == at) & (p2 > 0), dn_copy),
            ((p1 >= at) & (p1 < l1 - 1), out_up_copy),
            ((p1 <= at) & (p1 > 0), out_dn_copy),
        ):
            @pl.when(used)
            def _():
                copy(i).wait_send()

        return carry

    lax.fori_loop(0, chunks, drain, 0)

    def drain_result(m, carry):
        result_copy(m).wait()
        return carry

    lax.fori_loop(0, attends, drain_result, 0)


def solution(mesh):
    ring = mesh.shape["ctx"]

    def body(queries, new_keys, new_values, prefix_keys, prefix_values, pool_keys, pool_values, owners, lengths):
        heads = queries.shape[1] // HD
        kv_heads = new_keys.shape[1] // HD
        pieces = pool_keys.shape[1] * CUTS
        chunks = kv_heads * pieces
        c_rows = pool_keys.shape[2] // CUTS + prefix_keys.shape[0] * ring // pieces
        chunk_buf = pltpu.VMEM((chunks, c_rows, HD), jnp.bfloat16)
        vm = pl.BlockSpec(memory_space=pltpu.VMEM)
        hbm = pl.BlockSpec(memory_space=pl.ANY)
        sm = pl.BlockSpec(memory_space=pltpu.SMEM)
        return pl.pallas_call(
            functools.partial(kernel, ring, heads, kv_heads),
            out_shape=jax.ShapeDtypeStruct(queries.shape, jnp.bfloat16),
            in_specs=[hbm] + [vm] * 4 + [hbm] * 2 + [sm] * 2,
            out_specs=hbm,
            scratch_shapes=[chunk_buf] * 9
            + [
                pltpu.VMEM((2, chunks, c_rows, HD), jnp.bfloat16),
                pltpu.VMEM((queries.shape[0], queries.shape[0]), jnp.float32),
                pltpu.VMEM(queries.shape, jnp.bfloat16),
                pltpu.VMEM(queries.shape, jnp.bfloat16),
                pltpu.VMEM(pool_keys.shape, jnp.bfloat16),
                pltpu.VMEM(pool_values.shape, jnp.bfloat16),
                pltpu.SemaphoreType.DMA((8, chunks)),
                pltpu.SemaphoreType.DMA((8, chunks)),
                pltpu.SemaphoreType.DMA,
                pltpu.SemaphoreType.DMA((heads // HEADS_AT_ONCE,)),
                pltpu.SemaphoreType.DMA((2,)),
            ],
            compiler_params=pltpu.CompilerParams(
                collective_id=0, has_side_effects=True, vmem_limit_bytes=67043328
            ),
        )(queries, new_keys, new_values, prefix_keys, prefix_values, pool_keys, pool_values, owners, lengths)

    two = P(("groups", "ctx"), None)
    four = P(("groups", "ctx"), None, None, None)
    return jax.shard_map(
        body, mesh=mesh, in_specs=(two,) * 5 + (four,) * 2 + (P("groups"), P(("groups", "ctx"))),
        out_specs=two, check_vma=False,
    )
```
